32 devices in a mesh: tm: 4 (over z), space: 8 (over y, x, core).
Axes of the slice: x: 2, y: 2, z: 4, core: 2. Of those that a mesh axis runs over, the one named last changes fastest.
Arguments:
- thickness: float32 [4, 256, 2048], P('tm', 'space'), may hold values from 0 to 2
- bed_class: int32 [256, 2048], P('space'), may hold values from 0 to 15
- ice_mask: int32 [256, 2048], P('space'), may hold values 0 or 1
- zone_index: int32 [256, 2048], P('space'), may hold values from 0 to 7
- bed_levels: float32 [16], replicated, may hold values from -1 to 1
- balance_rates: float32 [8], replicated, may hold values from -0.3 to 0.3
Outputs:
- end_state: float32 [4, 256, 2048], P('tm', 'space')
- next_start: float32 [4, 256, 2048], P('tm', 'space')
The draws below stay inside these ranges and needn't reach their ends.
All inputs are finite; a program needn't handle non-finite values. No bound on the sum of `ice_mask` on one device may be relied on, other than what follows from the above.
Results may differ from the reference program's by a relative error of at most 0.0001.
Values sent between devices are 32-bit elements; how exact they have to be, the bound alone decides.
A program may use at most 128 MiB of HBM per device.

```python
import jax
import jax.numpy as jnp

NY = 2048
FSTEPS = 4
CSTEPS = 2
NCLASS = 16
NZONE = 8
SLICES = 4
NX = 256
N_TM = 4


def with_ends(values, stream_key, least, largest):
    shape = values.shape
    place = [jax.random.randint(jax.random.fold_in(stream_key, axis), (), 0, shape[axis]) for axis in range(len(shape))]
    values = values.at[tuple(place)].set(least)
    longest = shape.index(max(shape))
    place[longest] = (place[longest] + 1) % shape[longest]
    return values.at[tuple(place)].set(largest)


def steps_of(stream_key, dims, cuts, low, largest):
    gain, own = 1.0, jax.random.fold_in(stream_key, 6)
    for position, shards_of in cuts:
        draws = jnp.exp(jax.random.uniform(jax.random.fold_in(own, position), (shards_of,), jnp.float32, low / len(cuts), largest / len(cuts)))
        gain = gain * jnp.repeat(draws, dims[position] // shards_of).reshape([-1 if axis == position else 1 for axis in range(len(dims))])
    return gain


def setup_inputs(seed: int = 0) -> dict:
    splits = jax.random.split(jax.random.key(seed), 7)
    return {
        "thickness": jnp.clip(2.0 * jax.random.uniform(splits[0], (SLICES, NX, NY), jnp.float32) ** steps_of(splits[0], (SLICES, NX, NY), ((0, 4), (1, 8)), -0.2, 0.2), 0.0, 2.0),
        "bed_class": with_ends(jax.random.randint(splits[1], (NX, NY), 0, NCLASS), jax.random.fold_in(splits[1], 1), 0, NCLASS - 1).astype(jnp.int32),
        "ice_mask": with_ends((jax.random.randint(splits[2], (NX, NY), 0, 4) < 3).astype(jnp.int32), jax.random.fold_in(splits[2], 1), 0, 1),
        "zone_index": with_ends(jax.random.randint(splits[3], (NX, NY), 0, NZONE), jax.random.fold_in(splits[3], 1), 0, NZONE - 1).astype(jnp.int32),
        "bed_levels": jnp.clip(jax.random.uniform(splits[4], (NCLASS,), jnp.float32, -1.0, 1.0), -1.0, 1.0),
        "balance_rates": jnp.clip(jax.random.uniform(splits[5], (NZONE,), jnp.float32, -0.3, 0.3), -0.3, 0.3),
    }


glen_factor = 0.5
diff_cap = 1.0
time_step = 0.2


def lookup(index, table):
    result = jnp.zeros(index.shape, jnp.float32)
    for entry in range(table.shape[0]):
        result = result + jnp.where(index == entry, table[entry], jnp.float32(0.0))
    return result


def restrict(field):
    row_count, col_count = field.shape
    return field.reshape(row_count // 2, 2, col_count // 2, 2).mean(axis=(1, 3))


def prolong(field):
    return jnp.repeat(jnp.repeat(field, 2, axis=0), 2, axis=1)


def flow_step(thick, ground, cover, supply, spacing, tau):
    surface = ground + thick
    slope_x = (surface[2:, 1:-1] - surface[:-2, 1:-1]) / (2.0 * spacing)
    slope_y = (surface[1:-1, 2:] - surface[1:-1, :-2]) / (2.0 * spacing)
    inner = thick[1:-1, 1:-1]
    fifth = inner * inner
    fifth = fifth * fifth * inner
    diffusion = jnp.minimum(glen_factor * fifth * (slope_x * slope_x + slope_y * slope_y), diff_cap)
    level = surface[1:-1, 1:-1]
    flux_x = 0.5 * (diffusion[1:, :] + diffusion[:-1, :]) * (level[1:, :] - level[:-1, :]) / spacing
    flux_y = 0.5 * (diffusion[:, 1:] + diffusion[:, :-1]) * (level[:, 1:] - level[:, :-1]) / spacing
    flux_x = flux_x[:, 1:-1]
    flux_y = flux_y[1:-1, :]
    spread = (flux_x[1:, :] - flux_x[:-1, :] + flux_y[:, 1:] - flux_y[:, :-1]) / spacing
    updated = thick[2:-2, 2:-2] + tau * (spread + supply[2:-2, 2:-2])
    return jnp.maximum(updated, 0.0) * cover[2:-2, 2:-2]


def run_global(field, ground, cover, supply, count, spacing, tau):
    padding = ((2, 2), (2, 2))
    ground_pad = jnp.pad(ground, padding)
    cover_pad = jnp.pad(cover, padding)
    supply_pad = jnp.pad(supply, padding)
    for sweep in range(count):
        field = flow_step(jnp.pad(field, padding), ground_pad, cover_pad, supply_pad, spacing, tau)
    return field


def reference(thickness, bed_class, ice_mask, zone_index, bed_levels, balance_rates):
    ground = lookup(bed_class, bed_levels)
    supply = lookup(zone_index, balance_rates)
    cover = ice_mask.astype(jnp.float32)
    coarse_ground = restrict(ground)
    coarse_cover = restrict(cover)
    coarse_supply = restrict(supply)
    coarse_tau = time_step * FSTEPS / CSTEPS
    fine_ends = []
    previous = []
    jumps = []
    for member in range(N_TM):
        fine_end = run_global(thickness[member], ground, cover, supply, FSTEPS, 1.0, time_step)
        earlier = run_global(restrict(thickness[member]), coarse_ground, coarse_cover, coarse_supply, CSTEPS, 2.0, coarse_tau)
        fine_ends.append(fine_end)
        previous.append(earlier)
        jumps.append(restrict(fine_end) - earlier)
    current = restrict(thickness[0])
    ends = []
    for member in range(N_TM):
        propagated = run_global(current, coarse_ground, coarse_cover, coarse_supply, CSTEPS, 2.0, coarse_tau)
        ends.append(fine_ends[member] + prolong(propagated - previous[member]))
        current = propagated + jumps[member]
    end_state = jnp.stack(ends)
    next_start = jnp.concatenate([thickness[:1], end_state[:-1]], axis=0)
    return end_state, next_start
```

```python
import functools

import jax
import jax.numpy as jnp
from jax import lax
from jax.experimental import pallas as pl
from jax.experimental.pallas import tpu as pltpu
from jax.sharding import PartitionSpec as P

FSTEPS = 4
CSTEPS = 2
SUB = 8
LANE = 128
BLOCK = 8

glen_factor = 0.5
diff_cap = 1.0
time_step = 0.2

MESH = pl.DeviceIdType.MESH


def load(ref, start, count):
    width = ref.shape[-1]
    return [ref[pl.ds(start, count), :, v * LANE : (v + 1) * LANE] for v in range(width // LANE)]


def store(ref, start, parts):
    for v, part in enumerate(parts):
        ref[pl.ds(start, part.shape[0]), :, v * LANE : (v + 1) * LANE] = part


def zero_rows(ref, start, count):
    ref[start : start + count] = jnp.zeros((count,) + ref.shape[1:], ref.dtype)


def lanes_of(x):
    return lax.broadcasted_iota(jnp.int32, x.shape, 2)


def subs_of(x):
    return lax.broadcasted_iota(jnp.int32, x.shape, 1)


def col_prev(parts, by):
    rolled = [pltpu.roll(x, by, 2) for x in parts]
    out = []
    for v, x in enumerate(rolled):
        if v:
            carried = rolled[v - 1]
        else:
            carried = jnp.where(subs_of(x) == 0, 0.0, pltpu.roll(rolled[-1], 1, 1))
        out.append(jnp.where(lanes_of(x) < by, carried, x))
    return out


def col_next(parts, by):
    rolled = [pltpu.roll(x, LANE - by, 2) for x in parts]
    out = []
    for v, x in enumerate(rolled):
        if v + 1 < len(rolled):
            carried = rolled[v + 1]
        else:
            carried = jnp.where(subs_of(x) == SUB - 1, 0.0, pltpu.roll(rolled[0], SUB - 1, 1))
        out.append(jnp.where(lanes_of(x) >= LANE - by, carried, x))
    return out


def each(fn, *lists):
    return [fn(*items) for items in zip(*lists)]


def flow_block(h, g, cover, gain, by, spacing, tau):
    slope_scale = glen_factor / (4.0 * spacing * spacing)
    flux_scale = tau * 0.5 / (spacing * spacing)
    s = each(jnp.add, g, h)
    mid = [x[1:-1] for x in s]
    right, left = col_next(mid, by), col_prev(mid, by)
    diffusion = []
    for x, r, l, thick in zip(s, right, left, h):
        dx = x[2:] - x[:-2]
        dy = r - l
        inner = thick[1:-1]
        square = inner * inner
        fifth = square * square * inner
        diffusion.append(jnp.minimum((slope_scale * fifth) * (dx * dx + dy * dy), diff_cap))
    centre = [d[1:-1] for d in diffusion]
    d_right, d_left = col_next(centre, by), col_prev(centre, by)
    out = []
    for v in range(len(h)):
        level, d = mid[v], diffusion[v]
        flux_x = (d[1:] + d[:-1]) * (level[1:] - level[:-1])
        here = level[1:-1]
        up = (centre[v] + d_right[v]) * (right[v][1:-1] - here)
        down = (d_left[v] + centre[v]) * (here - left[v][1:-1])
        spread = (flux_x[1:] - flux_x[:-1]) + (up - down)
        updated = h[v][2:-2] + (flux_scale * spread + gain[v])
        out.append(jnp.maximum(updated, 0.0) * cover[v])
    return out


def sweep(src, dst, ground, cover, gain, margin, by, spacing, tau):
    total = src.shape[0]
    first, last = margin, total - margin

    def block(start, count):
        h = load(src, start - 2, count + 4)
        g = load(ground, start - 2, count + 4)
        c = load(cover, start, count)
        a = load(gain, start, count)
        store(dst, start, flow_block(h, g, c, a, by, spacing, tau))

    blocks, rest = divmod(last - first, BLOCK)

    def body(i, carry):
        block(first + i * BLOCK, BLOCK)
        return carry

    lax.fori_loop(0, blocks, body, 0)
    if rest:
        block(first + blocks * BLOCK, rest)


def lookup(index, table_ref):
    values = [table_ref[i] for i in range(table_ref.shape[0])]
    bit = 1
    while len(values) > 1:
        mask = (index & bit) != 0
        if len(values) % 2:
            values.append(values[-1])
        values = [jnp.where(mask, values[i + 1], values[i]) for i in range(0, len(values), 2)]
        bit *= 2
    return values[0]


def restrict(parts):
    out = []
    for x in parts:
        pairs = x.reshape((x.shape[0] // 2, 2) + x.shape[1:])
        y = pairs[:, 0] + pairs[:, 1]
        even = (lanes_of(y) & 1) == 0
        out.append((y + jnp.where(even, pltpu.roll(y, LANE - 1, 2), pltpu.roll(y, 1, 2))) * 0.25)
    return out


def prolong(parts):
    out = []
    for x in parts:
        twice = jnp.broadcast_to(x[:, None], (x.shape[0], 2) + x.shape[1:])
        out.append(twice.reshape((2 * x.shape[0],) + x.shape[1:]))
    return out


def pack(parts):
    out = []
    for x in parts:
        pairs = x.reshape((x.shape[0] // 2, 2) + x.shape[1:])
        top, low = pairs[:, 0], pairs[:, 1]
        out.append(jnp.where((lanes_of(top) & 1) == 0, top, low))
    return out


def unpack(parts):
    out = []
    for x in parts:
        even = (lanes_of(x) & 1) == 0
        top = jnp.where(even, x, pltpu.roll(x, 1, 2))
        low = jnp.where(even, pltpu.roll(x, LANE - 1, 2), x)
        both = jnp.concatenate([top[:, None], low[:, None]], axis=1)
        out.append(both.reshape((2 * x.shape[0],) + x.shape[1:]))
    return out


def kernel(
    thick_hbm, bed_hbm, ice_hbm, zone_hbm, levels_ref, rates_ref,
    end_hbm, next_hbm,
    ha, hb, hc, bedx, icex, zonex, ground, cover, gain,
    cga, cgb, prev, jump, cground, ccover, cgain,
    packed_in, packed_out, prev_end, end_buf, next_buf,
    load_sem, halo_send, halo_recv, chain_send, chain_recv, end_send, end_recv, out_sem,
):
    t, s = lax.axis_index("tm"), lax.axis_index("space")
    n_t, n_s = lax.axis_size("tm"), lax.axis_size("space")
    fh = 2 * FSTEPS
    ch = 2 * CSTEPS
    rows = thick_hbm.shape[1]
    width = ha.shape[2]
    crows = rows // 2
    coarse_tau = time_step * FSTEPS / CSTEPS

    has_up, has_low = s > 0, s < n_s - 1
    has_prev, has_next = t > 0, t < n_t - 1

    sources = (thick_hbm.at[0], bed_hbm, ice_hbm, zone_hbm)
    fields = (ha, bedx, icex, zonex)
    loads = []
    for f, (src, dst) in enumerate(zip(sources, fields)):
        for k in range(SUB):
            cp = pltpu.make_async_copy(
                src.at[:, k * width : (k + 1) * width], dst.at[fh : fh + rows, k, :], load_sem.at[f, k]
            )
            cp.start()
            loads.append(cp)

    partners = [
        (has_up, (t, s - 1)),
        (has_low, (t, s + 1)),
        (has_prev, (t - 1, s)),
        (has_next, (t + 1, s)),
        (has_prev & has_up, (t - 1, s - 1)),
        (has_prev & has_low, (t - 1, s + 1)),
        (has_next & has_up, (t + 1, s - 1)),
        (has_next & has_low, (t + 1, s + 1)),
    ]
    barrier = pltpu.get_barrier_semaphore()
    for cond, device in partners:
        @pl.when(cond)
        def _(device=device):
            pl.semaphore_signal(barrier, inc=1, device_id=device, device_id_type=MESH)
    sides = has_up.astype(jnp.int32) + has_low.astype(jnp.int32)
    slices = has_prev.astype(jnp.int32) + has_next.astype(jnp.int32)
    pl.semaphore_wait(barrier, sides + slices * (1 + sides))

    for cp in loads:
        cp.wait()

    def remote(src, dst, ssem, rsem, device):
        return pltpu.make_async_remote_copy(
            src_ref=src, dst_ref=dst, send_sem=ssem, recv_sem=rsem, device_id=device, device_id_type=MESH
        )

    def halo_copy(side, f):
        ref = fields[f]
        if side == 0:
            src, dst, device = ref.at[fh : 2 * fh], ref.at[fh + rows : 2 * fh + rows], (t, s - 1)
        else:
            src, dst, device = ref.at[rows : fh + rows], ref.at[0:fh], (t, s + 1)
        return remote(src, dst, halo_send.at[side, f], halo_recv.at[side, f], device)

    for side, cond in ((0, has_up), (1, has_low)):
        @pl.when(cond)
        def _(side=side):
            for f in range(len(fields)):
                halo_copy(side, f).start()

    def look_rows(start, count):
        store(ground, start, [lookup(x, levels_ref) for x in load(bedx, start, count)])
        store(gain, start, [time_step * lookup(x, rates_ref) for x in load(zonex, start, count)])
        store(cover, start, [x.astype(jnp.float32) for x in load(icex, start, count)])

    def coarsen(start, count):
        half, n = start // 2 if isinstance(start, int) else lax.div(start, 2), count // 2
        store(cground, half, restrict(load(ground, start, count)))
        store(ccover, half, restrict(load(cover, start, count)))
        store(cgain, half, [x * (coarse_tau / time_step) for x in restrict(load(gain, start, count))])
        store(cga, half, restrict(load(ha, start, count)))

    def own_rows(i, carry):
        start = fh + i * 8
        look_rows(start, 8)
        coarsen(start, 8)
        return carry

    lax.fori_loop(0, rows // 8, own_rows, 0)

    for side, cond, start in ((1, has_up, 0), (0, has_low, fh + rows)):
        @pl.when(cond)
        def _(side=side, start=start):
            for f in range(len(fields)):
                halo_copy(side, f).wait_recv()
            look_rows(start, fh)

        @pl.when(jnp.logical_not(cond))
        def _(start=start):
            for ref in (ha, ground, cover, gain):
                zero_rows(ref, start, fh)

        coarsen(start, fh)

    chain = (ha, hb, hc, hb, hc)
    for step in range(FSTEPS):
        sweep(chain[step], chain[step + 1], ground, cover, gain, 2 * (step + 1), 1, 1.0, time_step)
    fine = hc

    def end_copy():
        return remote(fine.at[fh : fh + rows], prev_end, end_send.at[0], end_recv.at[0], (t + 1, s))

    def chain_copy(part, slot):
        n, m = ch // 2, crows // 2
        src = (packed_out, packed_out.at[0:n], packed_out.at[m - n : m])[part]
        low, high = ((n, n + m), (n + m, 2 * n + m), (0, n))[part]
        dst = packed_in.at[low:high]
        return remote(src, dst, chain_send.at[part], chain_recv.at[part], (slot, (s, s - 1, s + 1)[part]))

    chain_conds = (has_next, has_next & has_up, has_next & has_low)

    def coarse_run(src, tmp, dst):
        sweep(src, tmp, cground, ccover, cgain, 2, 2, 2.0, coarse_tau)
        sweep(tmp, dst, cground, ccover, cgain, 4, 2, 2.0, coarse_tau)

    coarse_run(cga, cgb, prev)

    def jump_rows(i, carry):
        fine_mean = restrict(load(fine, fh + 8 * i, 8))
        store(jump, ch + 4 * i, each(jnp.subtract, fine_mean, load(prev, ch + 4 * i, 4)))
        return carry

    lax.fori_loop(0, rows // 8, jump_rows, 0)

    @pl.when(has_next & has_prev)
    def _():
        end_copy().start()

    @pl.when(has_prev)
    def _():
        n, m = ch // 2, crows // 2
        chain_copy(0, t - 1).wait_recv()
        store(cga, ch, unpack(load(packed_in, n, m)))

        @pl.when(has_low)
        def _():
            chain_copy(1, t - 1).wait_recv()
            store(cga, ch + crows, unpack(load(packed_in, n + m, n)))

        @pl.when(has_up)
        def _():
            chain_copy(2, t - 1).wait_recv()
            store(cga, 0, unpack(load(packed_in, 0, n)))

        @pl.when(jnp.logical_not(has_low))
        def _():
            zero_rows(cga, ch + crows, ch)

        @pl.when(jnp.logical_not(has_up))
        def _():
            zero_rows(cga, 0, ch)

        coarse_run(cga, cgb, prev)

    def current_rows(i, carry):
        row = ch + 4 * i
        value = each(jnp.add, load(prev, row, 4), load(jump, row, 4))
        store(cgb, row, value)
        store(packed_out, 2 * i, pack(value))
        return carry

    lax.fori_loop(0, crows // 4, current_rows, 0)

    for part, cond in enumerate(chain_conds):
        @pl.when(cond)
        def _(part=part):
            chain_copy(part, t + 1).start()

    @pl.when(has_next & jnp.logical_not(has_prev))
    def _():
        end_copy().start()

    def finish(fine_ref, fine_at, current_ref, out_ref):
        def body(i, carry):
            e = load(fine_ref, fine_at + 8 * i, 8)
            diff = each(jnp.subtract, load(current_ref, ch + 4 * i, 4), restrict(e))
            store(out_ref, 8 * i, each(jnp.add, e, prolong(diff)))
            return carry

        lax.fori_loop(0, rows // 8, body, 0)

    def write_out(buf, at, out, slot):
        return [
            pltpu.make_async_copy(
                buf.at[at : at + rows, k, :], out.at[0, :, k * width : (k + 1) * width], out_sem.at[slot, k]
            )
            for k in range(SUB)
        ]

    finish(fine, fh, cgb, end_buf)
    end_writes = write_out(end_buf, 0, end_hbm, 0)
    for cp in end_writes:
        cp.start()

    @pl.when(has_prev)
    def _():
        remote(fine.at[fh : fh + rows], prev_end, end_send.at[0], end_recv.at[0], (t - 1, s)).wait_recv()
        finish(prev_end, 0, cga, next_buf)

    @pl.when(jnp.logical_not(has_prev))
    def _():
        next_buf[...] = ha[fh : fh + rows]

    next_writes = write_out(next_buf, 0, next_hbm, 1)
    for cp in next_writes:
        cp.start()

    for side, cond in ((0, has_up), (1, has_low)):
        @pl.when(cond)
        def _(side=side):
            for f in range(len(fields)):
                halo_copy(side, f).wait_send()
    for part, cond in enumerate(chain_conds):
        @pl.when(cond)
        def _(part=part):
            chain_copy(part, t + 1).wait_send()

    @pl.when(has_next)
    def _():
        end_copy().wait_send()

    for cp in end_writes + next_writes:
        cp.wait()


def per_device(thickness, bed_class, ice_mask, zone_index, bed_levels, balance_rates):
    _, rows, cols = thickness.shape
    width = cols // SUB
    crows = rows // 2
    fx, cx = rows + 4 * FSTEPS, crows + 4 * CSTEPS

    def buf(count, dtype=jnp.float32):
        return pltpu.VMEM((count, SUB, width), dtype)

    dma = pltpu.SemaphoreType.DMA
    shape = jax.ShapeDtypeStruct(thickness.shape, jnp.float32)
    return pl.pallas_call(
        kernel,
        out_shape=(shape, shape),
        in_specs=[pl.BlockSpec(memory_space=pl.ANY)] * 4 + [pl.BlockSpec(memory_space=pltpu.SMEM)] * 2,
        out_specs=(pl.BlockSpec(memory_space=pl.ANY), pl.BlockSpec(memory_space=pl.ANY)),
        scratch_shapes=[
            buf(fx), buf(fx), buf(fx),
            buf(fx, jnp.int32), buf(fx, jnp.int32), buf(fx, jnp.int32),
            buf(fx), buf(fx), buf(fx),
            buf(cx), buf(cx), buf(cx), buf(cx), buf(cx), buf(cx), buf(cx),
            buf(cx // 2), buf(crows // 2), buf(rows), buf(rows), buf(rows),
            dma((4, SUB)), dma((2, 4)), dma((2, 4)), dma((3,)), dma((3,)), dma((1,)), dma((1,)), dma((2, SUB)),
        ],
        compiler_params=pltpu.CompilerParams(collective_id=0, has_side_effects=True),
    )(thickness, bed_class, ice_mask, zone_index, bed_levels, balance_rates)


def solution(mesh):
    placed = (
        P("tm", "space", None),
        P("space", None),
        P("space", None),
        P("space", None),
        P(),
        P(),
    )
    return jax.shard_map(
        per_device,
        mesh=mesh,
        in_specs=placed,
        out_specs=(P("tm", "space", None), P("tm", "space", None)),
        check_vma=False,
    )
```

```python
import functools

import jax
import jax.numpy as jnp
from jax import lax
from jax.experimental import pallas as pl
from jax.experimental.pallas import tpu as pltpu
from jax.sharding import PartitionSpec as P

FSTEPS = 4
CSTEPS = 2
SUB = 8
LANE = 128
BLOCK = 8

glen_factor = 0.5
diff_cap = 1.0
time_step = 0.2

MESH = pl.DeviceIdType.MESH


def load(ref, start, count):
    width = ref.shape[-1]
    return [ref[pl.ds(start, count), :, v * LANE : (v + 1) * LANE] for v in range(width // LANE)]


def store(ref, start, parts):
    for v, part in enumerate(parts):
        ref[pl.ds(start, part.shape[0]), :, v * LANE : (v + 1) * LANE] = part


def zero_rows(ref, start, count):
    ref[start : start + count] = jnp.zeros((count,) + ref.shape[1:], ref.dtype)


def lanes_of(x):
    return lax.broadcasted_iota(jnp.int32, x.shape, 2)


def subs_of(x):
    return lax.broadcasted_iota(jnp.int32, x.shape, 1)


def col_prev(parts, by):
    rolled = [pltpu.roll(x, by, 2) for x in parts]
    out = []
    for v, x in enumerate(rolled):
        if v:
            carried = rolled[v - 1]
        else:
            carried = jnp.where(subs_of(x) == 0, 0.0, pltpu.roll(rolled[-1], 1, 1))
        out.append(jnp.where(lanes_of(x) < by, carried, x))
    return out


def col_next(parts, by):
    rolled = [pltpu.roll(x, LANE - by, 2) for x in parts]
    out = []
    for v, x in enumerate(rolled):
        if v + 1 < len(rolled):
            carried = rolled[v + 1]
        else:
            carried = jnp.where(subs_of(x) == SUB - 1, 0.0, pltpu.roll(rolled[0], SUB - 1, 1))
        out.append(jnp.where(lanes_of(x) >= LANE - by, carried, x))
    return out


def each(fn, *lists):
    return [fn(*items) for items in zip(*lists)]


def flow_block(h, g, cover, gain, by, spacing, tau):
    slope_scale = glen_factor / (4.0 * spacing * spacing)
    flux_scale = tau * 0.5 / (spacing * spacing)
    s = each(jnp.add, g, h)
    mid = [x[1:-1] for x in s]
    right, left = col_next(mid, by), col_prev(mid, by)
    diffusion = []
    for x, r, l, thick in zip(s, right, left, h):
        dx = x[2:] - x[:-2]
        dy = r - l
        inner = thick[1:-1]
        square = inner * inner
        fifth = square * square * inner
        diffusion.append(jnp.minimum((slope_scale * fifth) * (dx * dx + dy * dy), diff_cap))
    centre = [d[1:-1] for d in diffusion]
    d_right, d_left = col_next(centre, by), col_prev(centre, by)
    out = []
    for v in range(len(h)):
        level, d = mid[v], diffusion[v]
        flux_x = (d[1:] + d[:-1]) * (level[1:] - level[:-1])
        here = level[1:-1]
        up = (centre[v] + d_right[v]) * (right[v][1:-1] - here)
        down = (d_left[v] + centre[v]) * (here - left[v][1:-1])
        spread = (flux_x[1:] - flux_x[:-1]) + (up - down)
        updated = h[v][2:-2] + (flux_scale * spread + gain[v])
        out.append(jnp.maximum(updated, 0.0) * cover[v])
    return out


def sweep(src, dst, ground, cover, gain, first, rows, by, spacing, tau):
    def block(start, count):
        h = load(src, start - 2, count + 4)
        g = load(ground, start - 2, count + 4)
        c = load(cover, start, count)
        a = load(gain, start, count)
        store(dst, start, flow_block(h, g, c, a, by, spacing, tau))

    blocks, rest = divmod(rows, BLOCK)

    def body(i, carry):
        block(first + i * BLOCK, BLOCK)
        return carry

    if blocks == 1:
        block(first, BLOCK)
    elif blocks:
        lax.fori_loop(0, blocks, body, 0)
    if rest:
        block(first + blocks * BLOCK, rest)


def lookup(index, table_ref):
    values = [table_ref[i] for i in range(table_ref.shape[0])]
    bit = 1
    while len(values) > 1:
        mask = (index & bit) != 0
        if len(values) % 2:
            values.append(values[-1])
        values = [jnp.where(mask, values[i + 1], values[i]) for i in range(0, len(values), 2)]
        bit *= 2
    return values[0]


def restrict(parts):
    out = []
    for x in parts:
        pairs = x.reshape((x.shape[0] // 2, 2) + x.shape[1:])
        y = pairs[:, 0] + pairs[:, 1]
        even = (lanes_of(y) & 1) == 0
        out.append((y + jnp.where(even, pltpu.roll(y, LANE - 1, 2), pltpu.roll(y, 1, 2))) * 0.25)
    return out


def prolong(parts):
    out = []
    for x in parts:
        twice = jnp.broadcast_to(x[:, None], (x.shape[0], 2) + x.shape[1:])
        out.append(twice.reshape((2 * x.shape[0],) + x.shape[1:]))
    return out


def pack(parts):
    out = []
    for x in parts:
        pairs = x.reshape((x.shape[0] // 2, 2) + x.shape[1:])
        top, low = pairs[:, 0], pairs[:, 1]
        out.append(jnp.where((lanes_of(top) & 1) == 0, top, low))
    return out


def unpack(parts):
    out = []
    for x in parts:
        even = (lanes_of(x) & 1) == 0
        top = jnp.where(even, x, pltpu.roll(x, 1, 2))
        low = jnp.where(even, pltpu.roll(x, LANE - 1, 2), x)
        both = jnp.concatenate([top[:, None], low[:, None]], axis=1)
        out.append(both.reshape((2 * x.shape[0],) + x.shape[1:]))
    return out


def kernel(
    thick_hbm, bed_hbm, ice_hbm, zone_hbm, levels_ref, rates_ref,
    end_hbm, next_hbm,
    ha, hb, hc, bedx, icex, zonex, ground, cover, gain,
    cga, cgb, prev, jump, cground, ccover, cgain,
    packed_in, packed_out, prev_end, end_buf, next_buf,
    load_sem, halo_send, halo_recv, chain_send, chain_recv, end_send, end_recv, out_sem,
):
    t, s = lax.axis_index("tm"), lax.axis_index("space")
    n_t, n_s = lax.axis_size("tm"), lax.axis_size("space")
    fh = 2 * FSTEPS
    ch = 2 * CSTEPS
    rows = thick_hbm.shape[1]
    width = ha.shape[2]
    crows = rows // 2
    coarse_tau = time_step * FSTEPS / CSTEPS

    has_up, has_low = s > 0, s < n_s - 1
    has_prev, has_next = t > 0, t < n_t - 1

    sources = (thick_hbm.at[0], bed_hbm, ice_hbm, zone_hbm)
    fields = (ha, bedx, icex, zonex)
    loads = []
    for f, (src, dst) in enumerate(zip(sources, fields)):
        for k in range(SUB):
            cp = pltpu.make_async_copy(
                src.at[:, k * width : (k + 1) * width], dst.at[fh : fh + rows, k, :], load_sem.at[f, k]
            )
            cp.start()
            loads.append(cp)

    partners = [
        (has_up, (t, s - 1)),
        (has_low, (t, s + 1)),
        (has_prev, (t - 1, s)),
        (has_next, (t + 1, s)),
        (has_prev & has_up, (t - 1, s - 1)),
        (has_prev & has_low, (t - 1, s + 1)),
        (has_next & has_up, (t + 1, s - 1)),
        (has_next & has_low, (t + 1, s + 1)),
    ]
    barrier = pltpu.get_barrier_semaphore()
    for cond, device in partners:
        @pl.when(cond)
        def _(device=device):
            pl.semaphore_signal(barrier, inc=1, device_id=device, device_id_type=MESH)
    sides = has_up.astype(jnp.int32) + has_low.astype(jnp.int32)
    slices = has_prev.astype(jnp.int32) + has_next.astype(jnp.int32)
    pl.semaphore_wait(barrier, sides + slices * (1 + sides))

    for cp in loads:
        cp.wait()

    def remote(src, dst, ssem, rsem, device):
        return pltpu.make_async_remote_copy(
            src_ref=src, dst_ref=dst, send_sem=ssem, recv_sem=rsem, device_id=device, device_id_type=MESH
        )

    depth = (fh, fh, fh - 2, fh - 2)

    def halo_copy(side, f):
        ref, n = fields[f], depth[f]
        if side == 0:
            src, dst, device = ref.at[fh : fh + n], ref.at[fh + rows : fh + rows + n], (t, s - 1)
        else:
            src, dst, device = ref.at[fh + rows - n : fh + rows], ref.at[fh - n : fh], (t, s + 1)
        return remote(src, dst, halo_send.at[side, f], halo_recv.at[side, f], device)

    for side, cond in ((0, has_up), (1, has_low)):
        @pl.when(cond)
        def _(side=side):
            for f in range(len(fields)):
                halo_copy(side, f).start()

    def look_rows(start, count):
        store(ground, start, [lookup(x, levels_ref) for x in load(bedx, start, count)])
        store(gain, start, [time_step * lookup(x, rates_ref) for x in load(zonex, start, count)])
        store(cover, start, [x.astype(jnp.float32) for x in load(icex, start, count)])

    def coarsen(start, count):
        half = start // 2 if isinstance(start, int) else lax.div(start, 2)
        store(cground, half, restrict(load(ground, start, count)))
        store(ccover, half, restrict(load(cover, start, count)))
        store(cgain, half, [x * (coarse_tau / time_step) for x in restrict(load(gain, start, count))])
        store(cga, half, restrict(load(ha, start, count)))

    chain = (ha, hb, hc, hb, hc)
    fine = hc

    def fine_sweep(step, first, count):
        sweep(chain[step], chain[step + 1], ground, cover, gain, first, count, 1, 1.0, time_step)

    def coarse_sweep(src, dst, first, count):
        sweep(src, dst, cground, ccover, cgain, first, count, 2, 2.0, coarse_tau)

    def jump_rows(row, count):
        fine_mean = restrict(load(fine, 2 * row, 2 * count))
        store(jump, row, each(jnp.subtract, fine_mean, load(prev, row, count)))

    def own_rows(i, carry):
        start = fh + i * 8
        look_rows(start, 8)
        coarsen(start, 8)
        return carry

    lax.fori_loop(0, rows // 8, own_rows, 0)

    for step in range(FSTEPS):
        edge = 2 * (step + 1)
        fine_sweep(step, fh + edge, rows - 2 * edge)
    coarse_sweep(cga, cgb, ch + 2, crows - 4)
    coarse_sweep(cgb, prev, ch + 4, crows - 8)
    jump_rows(2 * ch, crows - 2 * ch)

    def one_side(j, carry):
        side = lax.rem(s + j, 2)
        upper = side == 1

        def pick(up, low):
            return jnp.where(upper, up, low)

        start = pick(0, fh + rows)
        there = (upper & has_up) | (jnp.logical_not(upper) & has_low)

        @pl.when(there)
        def _():
            for f in range(len(fields)):
                n = depth[f]
                ref = fields[f].at[pl.ds(pick(fh - n, fh + rows), n)]
                remote(ref, ref, halo_send.at[side, f], halo_recv.at[side, f], (t, pick(s - 1, s + 1))).wait_recv()
            look_rows(start, fh)

        @pl.when(jnp.logical_not(there))
        def _():
            for ref in (ha, ground, cover, gain):
                zero = jnp.zeros((fh, SUB, LANE), ref.dtype)
                store(ref, start, [zero] * (width // LANE))

        coarsen(start, fh)
        for step in range(FSTEPS):
            edge = 2 * (step + 1)
            fine_sweep(step, pick(edge, fh + rows - edge), fh)
        coarse_sweep(cga, cgb, pick(2, ch + crows - 2), ch)
        coarse_sweep(cgb, prev, pick(4, ch + crows - 4), ch)
        jump_rows(pick(ch, crows), ch)
        return carry

    lax.fori_loop(0, 2, one_side, 0)

    def end_copy():
        return remote(fine.at[fh : fh + rows], prev_end, end_send.at[0], end_recv.at[0], (t + 1, s))

    def chain_copy(part, slot):
        n, m = ch // 2, crows // 2
        src = (packed_out, packed_out.at[0:n], packed_out.at[m - n : m])[part]
        low, high = ((n, n + m), (n + m, 2 * n + m), (0, n))[part]
        dst = packed_in.at[low:high]
        return remote(src, dst, chain_send.at[part], chain_recv.at[part], (slot, (s, s - 1, s + 1)[part]))

    chain_conds = (has_next, has_next & has_up, has_next & has_low)

    def coarse_run(src, tmp, dst):
        coarse_sweep(src, tmp, 2, crows + 2 * ch - 4)
        coarse_sweep(tmp, dst, ch, crows)

    @pl.when(has_next & has_prev)
    def _():
        end_copy().start()

    @pl.when(has_prev)
    def _():
        n, m = ch // 2, crows // 2
        chain_copy(0, t - 1).wait_recv()
        store(cga, ch, unpack(load(packed_in, n, m)))

        @pl.when(has_low)
        def _():
            chain_copy(1, t - 1).wait_recv()
            store(cga, ch + crows, unpack(load(packed_in, n + m, n)))

        @pl.when(has_up)
        def _():
            chain_copy(2, t - 1).wait_recv()
            store(cga, 0, unpack(load(packed_in, 0, n)))

        @pl.when(jnp.logical_not(has_low))
        def _():
            zero_rows(cga, ch + crows, ch)

        @pl.when(jnp.logical_not(has_up))
        def _():
            zero_rows(cga, 0, ch)

        coarse_run(cga, cgb, prev)

    def current_rows(i, carry):
        row = ch + 4 * i
        value = each(jnp.add, load(prev, row, 4), load(jump, row, 4))
        store(cgb, row, value)
        store(packed_out, 2 * i, pack(value))
        return carry

    lax.fori_loop(0, crows // 4, current_rows, 0)

    for part, cond in enumerate(chain_conds):
        @pl.when(cond)
        def _(part=part):
            chain_copy(part, t + 1).start()

    @pl.when(has_next & jnp.logical_not(has_prev))
    def _():
        end_copy().start()

    def finish(fine_ref, fine_at, current_ref, out_ref):
        def body(i, carry):
            e = load(fine_ref, fine_at + 8 * i, 8)
            diff = each(jnp.subtract, load(current_ref, ch + 4 * i, 4), restrict(e))
            store(out_ref, 8 * i, each(jnp.add, e, prolong(diff)))
            return carry

        lax.fori_loop(0, rows // 8, body, 0)

    def write_out(buf, at, out, slot):
        return [
            pltpu.make_async_copy(
                buf.at[at : at + rows, k, :], out.at[0, :, k * width : (k + 1) * width], out_sem.at[slot, k]
            )
            for k in range(SUB)
        ]

    finish(fine, fh, cgb, end_buf)
    end_writes = write_out(end_buf, 0, end_hbm, 0)
    for cp in end_writes:
        cp.start()

    @pl.when(has_prev)
    def _():
        remote(fine.at[fh : fh + rows], prev_end, end_send.at[0], end_recv.at[0], (t - 1, s)).wait_recv()
        finish(prev_end, 0, cga, next_buf)

    @pl.when(jnp.logical_not(has_prev))
    def _():
        next_buf[...] = ha[fh : fh + rows]

    next_writes = write_out(next_buf, 0, next_hbm, 1)
    for cp in next_writes:
        cp.start()

    for side, cond in ((0, has_up), (1, has_low)):
        @pl.when(cond)
        def _(side=side):
            for f in range(len(fields)):
                halo_copy(side, f).wait_send()
    for part, cond in enumerate(chain_conds):
        @pl.when(cond)
        def _(part=part):
            chain_copy(part, t + 1).wait_send()

    @pl.when(has_next)
    def _():
        end_copy().wait_send()

    for cp in end_writes + next_writes:
        cp.wait()


def per_device(thickness, bed_class, ice_mask, zone_index, bed_levels, balance_rates):
    _, rows, cols = thickness.shape
    width = cols // SUB
    crows = rows // 2
    fx, cx = rows + 4 * FSTEPS, crows + 4 * CSTEPS

    def buf(count, dtype=jnp.float32):
        return pltpu.VMEM((count, SUB, width), dtype)

    dma = pltpu.SemaphoreType.DMA
    shape = jax.ShapeDtypeStruct(thickness.shape, jnp.float32)
    return pl.pallas_call(
        kernel,
        out_shape=(shape, shape),
        in_specs=[pl.BlockSpec(memory_space=pl.ANY)] * 4 + [pl.BlockSpec(memory_space=pltpu.SMEM)] * 2,
        out_specs=(pl.BlockSpec(memory_space=pl.ANY), pl.BlockSpec(memory_space=pl.ANY)),
        scratch_shapes=[
            buf(fx), buf(fx), buf(fx),
            buf(fx, jnp.int32), buf(fx, jnp.int32), buf(fx, jnp.int32),
            buf(fx), buf(fx), buf(fx),
            buf(cx), buf(cx), buf(cx), buf(cx), buf(cx), buf(cx), buf(cx),
            buf(cx // 2), buf(crows // 2), buf(rows), buf(rows), buf(rows),
            dma((4, SUB)), dma((2, 4)), dma((2, 4)), dma((3,)), dma((3,)), dma((1,)), dma((1,)), dma((2, SUB)),
        ],
        compiler_params=pltpu.CompilerParams(collective_id=0, has_side_effects=True),
    )(thickness, bed_class, ice_mask, zone_index, bed_levels, balance_rates)


def solution(mesh):
    placed = (
        P("tm", "space", None),
        P("space", None),
        P("space", None),
        P("space", None),
        P(),
        P(),
    )
    return jax.shard_map(
        per_device,
        mesh=mesh,
        in_specs=placed,
        out_specs=(P("tm", "space", None), P("tm", "space", None)),
        check_vma=False,
    )
```

```python
import functools

import jax
import jax.numpy as jnp
from jax import lax
from jax.experimental import pallas as pl
from jax.experimental.pallas import tpu as pltpu
from jax.sharding import PartitionSpec as P

FSTEPS = 4
CSTEPS = 2
SUB = 8
LANE = 128
BLOCK = 8

glen_factor = 0.5
diff_cap = 1.0
time_step = 0.2

MESH = pl.DeviceIdType.MESH


def load(ref, start, count):
    width = ref.shape[-1]
    return [ref[pl.ds(start, count), :, v * LANE : (v + 1) * LANE] for v in range(width // LANE)]


def store(ref, start, parts):
    for v, part in enumerate(parts):
        ref[pl.ds(start, part.shape[0]), :, v * LANE : (v + 1) * LANE] = part


def zero_rows(ref, start, count):
    ref[start : start + count] = jnp.zeros((count,) + ref.shape[1:], ref.dtype)


def lanes_of(x):
    return lax.broadcasted_iota(jnp.int32, x.shape, 2)


def subs_of(x):
    return lax.broadcasted_iota(jnp.int32, x.shape, 1)


def col_prev(parts, by):
    rolled = [pltpu.roll(x, by, 2) for x in parts]
    out = []
    for v, x in enumerate(rolled):
        if v:
            carried = rolled[v - 1]
        else:
            carried = jnp.where(subs_of(x) == 0, 0.0, pltpu.roll(rolled[-1], 1, 1))
        out.append(jnp.where(lanes_of(x) < by, carried, x))
    return out


def col_next(parts, by):
    rolled = [pltpu.roll(x, LANE - by, 2) for x in parts]
    out = []
    for v, x in enumerate(rolled):
        if v + 1 < len(rolled):
            carried = rolled[v + 1]
        else:
            carried = jnp.where(subs_of(x) == SUB - 1, 0.0, pltpu.roll(rolled[0], SUB - 1, 1))
        out.append(jnp.where(lanes_of(x) >= LANE - by, carried, x))
    return out


def each(fn, *lists):
    return [fn(*items) for items in zip(*lists)]


def flow_block(h, g, cover, gain, by, spacing, tau):
    slope_scale = glen_factor / (4.0 * spacing * spacing)
    flux_scale = tau * 0.5 / (spacing * spacing)
    s = each(jnp.add, g, h)
    mid = [x[1:-1] for x in s]
    right, left = col_next(mid, by), col_prev(mid, by)
    diffusion = []
    for x, r, l, thick in zip(s, right, left, h):
        dx = x[2:] - x[:-2]
        dy = r - l
        inner = thick[1:-1]
        square = inner * inner
        fifth = square * square * inner
        diffusion.append(jnp.minimum((slope_scale * fifth) * (dx * dx + dy * dy), diff_cap))
    centre = [d[1:-1] for d in diffusion]
    d_right, d_left = col_next(centre, by), col_prev(centre, by)
    out = []
    for v in range(len(h)):
        level, d = mid[v], diffusion[v]
        flux_x = (d[1:] + d[:-1]) * (level[1:] - level[:-1])
        here = level[1:-1]
        up = (centre[v] + d_right[v]) * (right[v][1:-1] - here)
        down = (d_left[v] + centre[v]) * (here - left[v][1:-1])
        spread = (flux_x[1:] - flux_x[:-1]) + (up - down)
        updated = h[v][2:-2] + (flux_scale * spread + gain[v])
        out.append(jnp.maximum(updated, 0.0) * cover[v])
    return out


def sweep(src, dst, ground, cover, gain, first, rows, by, spacing, tau):
    def block(start, count):
        h = load(src, start - 2, count + 4)
        g = load(ground, start - 2, count + 4)
        c = load(cover, start, count)
        a = load(gain, start, count)
        store(dst, start, flow_block(h, g, c, a, by, spacing, tau))

    blocks, rest = divmod(rows, BLOCK)

    def body(i, carry):
        block(first + i * BLOCK, BLOCK)
        return carry

    if blocks == 1:
        block(first, BLOCK)
    elif blocks:
        lax.fori_loop(0, blocks, body, 0)
    if rest:
        block(first + blocks * BLOCK, rest)


def lookup(index, table_ref):
    values = [table_ref[i] for i in range(table_ref.shape[0])]
    bit = 1
    while len(values) > 1:
        mask = (index & bit) != 0
        if len(values) % 2:
            values.append(values[-1])
        values = [jnp.where(mask, values[i + 1], values[i]) for i in range(0, len(values), 2)]
        bit *= 2
    return values[0]


def restrict(parts):
    out = []
    for x in parts:
        pairs = x.reshape((x.shape[0] // 2, 2) + x.shape[1:])
        y = pairs[:, 0] + pairs[:, 1]
        even = (lanes_of(y) & 1) == 0
        out.append((y + jnp.where(even, pltpu.roll(y, LANE - 1, 2), pltpu.roll(y, 1, 2))) * 0.25)
    return out


def prolong(parts):
    out = []
    for x in parts:
        twice = jnp.broadcast_to(x[:, None], (x.shape[0], 2) + x.shape[1:])
        out.append(twice.reshape((2 * x.shape[0],) + x.shape[1:]))
    return out


def is_even(x):
    return (lanes_of(x) & 1) == 0


def to_odd(x):
    return pltpu.roll(x, 1, 2)


def to_even(x):
    return pltpu.roll(x, LANE - 1, 2)


def merge(evens, odds):
    return [jnp.where(is_even(x), x, y) for x, y in zip(evens, odds)]


def kernel(
    thick_hbm, bed_hbm, ice_hbm, zone_hbm, levels_ref, rates_ref,
    end_hbm, next_hbm,
    ha, hb, hc, bedx, icex, zonex, ground, cover, gain,
    cga, cgb, prev, jump, cground, ccover, cgain,
    pground, pcover, pgain, pjump, pcur, ptmp, pout, edge_out, edge_in, prev_end, end_buf, next_buf,
    load_sem, halo_send, halo_recv, chain_send, chain_recv, end_send, end_recv, out_sem, ready_sem,
):
    t, s = lax.axis_index("tm"), lax.axis_index("space")
    n_t, n_s = lax.axis_size("tm"), lax.axis_size("space")
    fh = 2 * FSTEPS
    ch = 2 * CSTEPS
    rows = thick_hbm.shape[1]
    width = ha.shape[2]
    crows = rows // 2
    half = crows // 2
    edge_rows = CSTEPS
    coarse_tau = time_step * FSTEPS / CSTEPS

    has_up, has_low = s > 0, s < n_s - 1
    has_prev, has_next = t > 0, t < n_t - 1

    sources = (thick_hbm.at[0], bed_hbm, ice_hbm, zone_hbm)
    fields = (ha, bedx, icex, zonex)
    loads = []
    for f, (src, dst) in enumerate(zip(sources, fields)):
        for k in range(SUB):
            cp = pltpu.make_async_copy(
                src.at[:, k * width : (k + 1) * width], dst.at[fh : fh + rows, k, :], load_sem.at[f, k]
            )
            cp.start()
            loads.append(cp)

    partners = [
        (has_up, (t, s - 1)),
        (has_low, (t, s + 1)),
        (has_prev, (t - 1, s)),
        (has_next, (t + 1, s)),
    ]
    barrier = pltpu.get_barrier_semaphore()
    for cond, device in partners:
        @pl.when(cond)
        def _(device=device):
            pl.semaphore_signal(barrier, inc=1, device_id=device, device_id_type=MESH)
    sides = has_up.astype(jnp.int32) + has_low.astype(jnp.int32)
    slices = has_prev.astype(jnp.int32) + has_next.astype(jnp.int32)
    pl.semaphore_wait(barrier, sides + slices)

    @pl.when(has_prev)
    def _():
        pl.semaphore_signal(ready_sem, inc=1, device_id=(t - 1, s), device_id_type=MESH)

    for cp in loads:
        cp.wait()

    def remote(src, dst, ssem, rsem, device):
        return pltpu.make_async_remote_copy(
            src_ref=src, dst_ref=dst, send_sem=ssem, recv_sem=rsem, device_id=device, device_id_type=MESH
        )

    depth = (fh, fh, fh - 2, fh - 2)

    def halo_copy(side, f):
        ref, n = fields[f], depth[f]
        if side == 0:
            src, dst, device = ref.at[fh : fh + n], ref.at[fh + rows : fh + rows + n], (t, s - 1)
        else:
            src, dst, device = ref.at[fh + rows - n : fh + rows], ref.at[fh - n : fh], (t, s + 1)
        return remote(src, dst, halo_send.at[side, f], halo_recv.at[side, f], device)

    for side, cond in ((0, has_up), (1, has_low)):
        @pl.when(cond)
        def _(side=side):
            for f in range(len(fields)):
                halo_copy(side, f).start()

    def look_rows(start, count):
        store(ground, start, [lookup(x, levels_ref) for x in load(bedx, start, count)])
        store(gain, start, [time_step * lookup(x, rates_ref) for x in load(zonex, start, count)])
        store(cover, start, [x.astype(jnp.float32) for x in load(icex, start, count)])

    def coarsen(start, count):
        half = start // 2 if isinstance(start, int) else lax.div(start, 2)
        store(cground, half, restrict(load(ground, start, count)))
        store(ccover, half, restrict(load(cover, start, count)))
        store(cgain, half, [x * (coarse_tau / time_step) for x in restrict(load(gain, start, count))])
        store(cga, half, restrict(load(ha, start, count)))

    chain = (ha, hb, hc, hb, hc)
    fine = hc

    def fine_sweep(step, first, count):
        sweep(chain[step], chain[step + 1], ground, cover, gain, first, count, 1, 1.0, time_step)

    def coarse_sweep(src, dst, first, count):
        sweep(src, dst, cground, ccover, cgain, first, count, 2, 2.0, coarse_tau)

    def jump_rows(row, count):
        fine_mean = restrict(load(fine, 2 * row, 2 * count))
        store(jump, row, each(jnp.subtract, fine_mean, load(prev, row, count)))

    def end_copy(piece, start, count, slot):
        return remote(
            fine.at[pl.ds(fh + start, count)], prev_end.at[pl.ds(start, count)],
            end_send.at[piece], end_recv.at[piece], (slot, s),
        )

    end_pieces = ((0, fh, rows - 2 * fh), (1, rows - fh, fh), (2, 0, fh))

    def own_rows(i, carry):
        start = fh + i * 8
        look_rows(start, 8)
        coarsen(start, 8)
        return carry

    lax.fori_loop(0, rows // 8, own_rows, 0)

    for step in range(FSTEPS):
        edge = 2 * (step + 1)
        fine_sweep(step, fh + edge, rows - 2 * edge)

    @pl.when(has_next)
    def _():
        end_copy(*end_pieces[0], t + 1).start()

    coarse_sweep(cga, cgb, ch + 2, crows - 4)
    coarse_sweep(cgb, prev, ch + 4, crows - 8)
    jump_rows(2 * ch, crows - 2 * ch)

    def one_side(j, carry):
        side = lax.rem(s + j, 2)
        upper = side == 1

        def pick(up, low):
            return jnp.where(upper, up, low)

        start = pick(0, fh + rows)
        there = (upper & has_up) | (jnp.logical_not(upper) & has_low)

        @pl.when(there)
        def _():
            for f in range(len(fields)):
                n = depth[f]
                ref = fields[f].at[pl.ds(pick(fh - n, fh + rows), n)]
                remote(ref, ref, halo_send.at[side, f], halo_recv.at[side, f], (t, pick(s - 1, s + 1))).wait_recv()
            look_rows(start, fh)

        @pl.when(jnp.logical_not(there))
        def _():
            for ref in (ha, ground, cover, gain):
                zero = jnp.zeros((fh, SUB, LANE), ref.dtype)
                store(ref, start, [zero] * (width // LANE))

        coarsen(start, fh)
        for step in range(FSTEPS):
            edge = 2 * (step + 1)
            fine_sweep(step, pick(edge, fh + rows - edge), fh)

        @pl.when(has_next & ((j == 0) | has_prev))
        def _():
            end_copy(1 + side, pick(0, rows - fh), fh, t + 1).start()

        coarse_sweep(cga, cgb, pick(2, ch + crows - 2), ch)
        coarse_sweep(cgb, prev, pick(4, ch + crows - 4), ch)
        jump_rows(pick(ch, crows), ch)
        return carry

    lax.fori_loop(0, 2, one_side, 0)

    def chain_copy(part, slot):
        src = (pout, edge_out.at[0], edge_out.at[1])[part]
        dst = (pcur.at[ch : ch + half], edge_in.at[0], edge_in.at[1])[part]
        return remote(src, dst, chain_send.at[part], chain_recv.at[part], (slot, (s, s - 1, s + 1)[part]))

    chain_conds = (has_next, has_next & has_up, has_next & has_low)

    def packed_rows(ref, row, count):
        return merge(load(ref, row, count), load(ref, row + half, count))

    store(pjump, 0, packed_rows(jump, ch, half))

    @pl.when(jnp.logical_not(has_prev))
    def _():
        store(ptmp, ch, packed_rows(prev, ch, half))

    @pl.when(has_prev)
    def _():
        for src, dst in ((cground, pground), (ccover, pcover), (cgain, pgain)):
            store(dst, 0, packed_rows(src, 0, half))
            store(dst, half, packed_rows(src, half, 2 * ch))

    def finish(fine_ref, fine_at, current_ref, current_at, out_ref):
        def body(i, carry):
            p = load(current_ref, current_at + 4 * i, 4)
            top = merge(p, [to_odd(x) for x in p])
            low = merge([to_even(x) for x in p], p)
            for current, at in ((top, 8 * i), (low, 2 * half + 8 * i)):
                e = load(fine_ref, fine_at + at, 8)
                diff = each(jnp.subtract, current, restrict(e))
                store(out_ref, at, each(jnp.add, e, prolong(diff)))
            return carry

        lax.fori_loop(0, half // 4, body, 0)

    def write_out(buf, at, out, slot):
        return [
            pltpu.make_async_copy(
                buf.at[at : at + rows, k, :], out.at[0, :, k * width : (k + 1) * width], out_sem.at[slot, k]
            )
            for k in range(SUB)
        ]

    next_writes = write_out(next_buf, 0, next_hbm, 1)

    def next_state():
        @pl.when(has_prev)
        def _():
            for piece in end_pieces:
                end_copy(*piece, t - 1).wait_recv()
            finish(prev_end, 0, pcur, ch, next_buf)

        @pl.when(jnp.logical_not(has_prev))
        def _():
            next_buf[...] = ha[fh : fh + rows]

        for cp in next_writes:
            cp.start()

    @pl.when(has_prev)
    def _():
        for part, cond in ((1, has_low), (2, has_up)):
            @pl.when(jnp.logical_not(cond))
            def _(part=part):
                edge_in[part - 1] = jnp.zeros(edge_in.shape[1:], jnp.float32)

        chain_copy(0, t - 1).wait_recv()
        for part, cond in ((1, has_low), (2, has_up)):
            @pl.when(cond)
            def _(part=part):
                chain_copy(part, t - 1).wait_recv()

        low, up = (load(edge_in.at[side], 0, edge_rows) for side in range(2))
        inner = load(pcur, half, ch)
        upper = [jnp.concatenate([x, to_even(x)], axis=0) for x in up]
        store(pcur, 0, merge(upper, [to_odd(x) for x in inner]))
        inner = load(pcur, ch, ch)
        lower = [jnp.concatenate([to_odd(x), x], axis=0) for x in low]
        store(pcur, ch + half, merge([to_even(x) for x in inner], lower))

        @pl.when(jnp.logical_not(has_next))
        def _():
            next_state()

        sweep(pcur, cgb, pground, pcover, pgain, 2, half + 2 * ch - 4, 2, 2.0, coarse_tau)
        sweep(cgb, ptmp, pground, pcover, pgain, ch, half, 2, 2.0, coarse_tau)

    value = each(jnp.add, load(ptmp, ch, half), load(pjump, 0, half))
    store(pout, 0, value)
    n = edge_rows
    store(edge_out.at[0], 0, merge([x[:n] for x in value], [to_odd(x[n : 2 * n]) for x in value]))
    store(edge_out.at[1], 0, merge([to_even(x[-2 * n : -n]) for x in value], [x[-n:] for x in value]))

    @pl.when(has_next)
    def _():
        pl.semaphore_wait(ready_sem, 1)

    for part, cond in enumerate(chain_conds):
        @pl.when(cond)
        def _(part=part):
            chain_copy(part, t + 1).start()

    last_side = lax.rem(s + 1, 2)

    @pl.when(has_next & jnp.logical_not(has_prev))
    def _():
        end_copy(1 + last_side, jnp.where(last_side == 1, 0, rows - fh), fh, t + 1).start()

    finish(fine, fh, pout, 0, end_buf)
    end_writes = write_out(end_buf, 0, end_hbm, 0)
    for cp in end_writes:
        cp.start()

    @pl.when(has_next)
    def _():
        next_state()

    for side, cond in ((0, has_up), (1, has_low)):
        @pl.when(cond)
        def _(side=side):
            for f in range(len(fields)):
                halo_copy(side, f).wait_send()
    for part, cond in enumerate(chain_conds):
        @pl.when(cond)
        def _(part=part):
            chain_copy(part, t + 1).wait_send()

    @pl.when(has_next)
    def _():
        for piece in end_pieces:
            end_copy(*piece, t + 1).wait_send()

    for cp in end_writes + next_writes:
        cp.wait()


def per_device(thickness, bed_class, ice_mask, zone_index, bed_levels, balance_rates):
    _, rows, cols = thickness.shape
    width = cols // SUB
    crows = rows // 2
    fx, cx, px = rows + 4 * FSTEPS, crows + 4 * CSTEPS, crows // 2 + 4 * CSTEPS

    def buf(count, dtype=jnp.float32):
        return pltpu.VMEM((count, SUB, width), dtype)

    dma = pltpu.SemaphoreType.DMA
    shape = jax.ShapeDtypeStruct(thickness.shape, jnp.float32)
    return pl.pallas_call(
        kernel,
        out_shape=(shape, shape),
        in_specs=[pl.BlockSpec(memory_space=pl.ANY)] * 4 + [pl.BlockSpec(memory_space=pltpu.SMEM)] * 2,
        out_specs=(pl.BlockSpec(memory_space=pl.ANY), pl.BlockSpec(memory_space=pl.ANY)),
        scratch_shapes=[
            buf(fx), buf(fx), buf(fx),
            buf(fx, jnp.int32), buf(fx, jnp.int32), buf(fx, jnp.int32),
            buf(fx), buf(fx), buf(fx),
            buf(cx), buf(cx), buf(cx), buf(cx), buf(cx), buf(cx), buf(cx),
            buf(px), buf(px), buf(px), buf(crows // 2), buf(px), buf(px), buf(crows // 2),
            pltpu.VMEM((2, CSTEPS, SUB, width), jnp.float32), pltpu.VMEM((2, CSTEPS, SUB, width), jnp.float32),
            buf(rows), buf(rows), buf(rows),
            dma((4, SUB)), dma((2, 4)), dma((2, 4)), dma((3,)), dma((3,)), dma((3,)), dma((3,)), dma((2, SUB)), pltpu.SemaphoreType.REGULAR,
        ],
        compiler_params=pltpu.CompilerParams(collective_id=0, has_side_effects=True),
    )(thickness, bed_class, ice_mask, zone_index, bed_levels, balance_rates)


def solution(mesh):
    placed = (
        P("tm", "space", None),
        P("space", None),
        P("space", None),
        P("space", None),
        P(),
        P(),
    )
    return jax.shard_map(
        per_device,
        mesh=mesh,
        in_specs=placed,
        out_specs=(P("tm", "space", None), P("tm", "space", None)),
        check_vma=False,
    )
```

```python
import functools

import jax
import jax.numpy as jnp
from jax import lax
from jax.experimental import pallas as pl
from jax.experimental.pallas import tpu as pltpu
from jax.sharding import PartitionSpec as P

FSTEPS = 4
CSTEPS = 2
SUB = 8
LANE = 128
BLOCK = 8

glen_factor = 0.5
diff_cap = 1.0
time_step = 0.2

MESH = pl.DeviceIdType.MESH


def load(ref, start, count):
    width = ref.shape[-1]
    return [ref[pl.ds(start, count), :, v * LANE : (v + 1) * LANE] for v in range(width // LANE)]


def store(ref, start, parts):
    for v, part in enumerate(parts):
        ref[pl.ds(start, part.shape[0]), :, v * LANE : (v + 1) * LANE] = part


def zero_rows(ref, start, count):
    ref[start : start + count] = jnp.zeros((count,) + ref.shape[1:], ref.dtype)


def lanes_of(x):
    return lax.broadcasted_iota(jnp.int32, x.shape, 2)


def subs_of(x):
    return lax.broadcasted_iota(jnp.int32, x.shape, 1)


def col_prev(parts, by):
    rolled = [pltpu.roll(x, by, 2) for x in parts]
    out = []
    for v, x in enumerate(rolled):
        if v:
            carried = rolled[v - 1]
        else:
            carried = jnp.where(subs_of(x) == 0, 0.0, pltpu.roll(rolled[-1], 1, 1))
        out.append(jnp.where(lanes_of(x) < by, carried, x))
    return out


def col_next(parts, by):
    rolled = [pltpu.roll(x, LANE - by, 2) for x in parts]
    out = []
    for v, x in enumerate(rolled):
        if v + 1 < len(rolled):
            carried = rolled[v + 1]
        else:
            carried = jnp.where(subs_of(x) == SUB - 1, 0.0, pltpu.roll(rolled[0], SUB - 1, 1))
        out.append(jnp.where(lanes_of(x) >= LANE - by, carried, x))
    return out


def each(fn, *lists):
    return [fn(*items) for items in zip(*lists)]


def flow_block(h, g, cover, gain, by, spacing, tau):
    slope_scale = glen_factor / (4.0 * spacing * spacing)
    flux_scale = tau * 0.5 / (spacing * spacing)
    s = each(jnp.add, g, h)
    mid = [x[1:-1] for x in s]
    right, left = col_next(mid, by), col_prev(mid, by)
    diffusion = []
    for x, r, l, thick in zip(s, right, left, h):
        dx = x[2:] - x[:-2]
        dy = r - l
        inner = thick[1:-1]
        square = inner * inner
        fifth = square * square * inner
        diffusion.append(jnp.minimum((slope_scale * fifth) * (dx * dx + dy * dy), diff_cap))
    centre = [d[1:-1] for d in diffusion]
    d_right, d_left = col_next(centre, by), col_prev(centre, by)
    out = []
    for v in range(len(h)):
        level, d = mid[v], diffusion[v]
        flux_x = (d[1:] + d[:-1]) * (level[1:] - level[:-1])
        here = level[1:-1]
        up = (centre[v] + d_right[v]) * (right[v][1:-1] - here)
        down = (d_left[v] + centre[v]) * (here - left[v][1:-1])
        spread = (flux_x[1:] - flux_x[:-1]) + (up - down)
        updated = h[v][2:-2] + (flux_scale * spread + gain[v])
        out.append(jnp.maximum(updated, 0.0) * cover[v])
    return out


def sweep(src, dst, ground, cover, gain, first, rows, by, spacing, tau):
    def block(start, count):
        h = load(src, start - 2, count + 4)
        g = load(ground, start - 2, count + 4)
        c = load(cover, start, count)
        a = load(gain, start, count)
        store(dst, start, flow_block(h, g, c, a, by, spacing, tau))

    blocks, rest = divmod(rows, BLOCK)

    def body(i, carry):
        block(first + i * BLOCK, BLOCK)
        return carry

    if blocks == 1:
        block(first, BLOCK)
    elif blocks:
        lax.fori_loop(0, blocks, body, 0)
    if rest:
        block(first + blocks * BLOCK, rest)


def lookup(index, table_ref):
    values = [table_ref[i] for i in range(table_ref.shape[0])]
    bit = 1
    while len(values) > 1:
        mask = (index & bit) != 0
        if len(values) % 2:
            values.append(values[-1])
        values = [jnp.where(mask, values[i + 1], values[i]) for i in range(0, len(values), 2)]
        bit *= 2
    return values[0]


def restrict(parts):
    out = []
    for x in parts:
        pairs = x.reshape((x.shape[0] // 2, 2) + x.shape[1:])
        y = pairs[:, 0] + pairs[:, 1]
        even = (lanes_of(y) & 1) == 0
        out.append((y + jnp.where(even, pltpu.roll(y, LANE - 1, 2), pltpu.roll(y, 1, 2))) * 0.25)
    return out


def prolong(parts):
    out = []
    for x in parts:
        twice = jnp.broadcast_to(x[:, None], (x.shape[0], 2) + x.shape[1:])
        out.append(twice.reshape((2 * x.shape[0],) + x.shape[1:]))
    return out


def is_even(x):
    return (lanes_of(x) & 1) == 0


def to_odd(x):
    return pltpu.roll(x, 1, 2)


def to_even(x):
    return pltpu.roll(x, LANE - 1, 2)


def merge(evens, odds):
    return [jnp.where(is_even(x), x, y) for x, y in zip(evens, odds)]


def kernel(
    thick_hbm, bed_hbm, ice_hbm, zone_hbm, levels_ref, rates_ref,
    end_hbm, next_hbm,
    ha, hb, hc, bedx, icex, zonex, ground, cover, gain,
    cga, cgb, prev, jump, cground, ccover, cgain,
    pground, pcover, pgain, pjump, pcur, ptmp, pout, edge_out, edge_in, prev_end, end_buf, next_buf,
    load_sem, halo_send, halo_recv, chain_send, chain_recv, end_send, end_recv, out_sem, ready_sem,
):
    t, s = lax.axis_index("tm"), lax.axis_index("space")
    n_t, n_s = lax.axis_size("tm"), lax.axis_size("space")
    fh = 2 * FSTEPS
    ch = 2 * CSTEPS
    rows = thick_hbm.shape[1]
    width = ha.shape[2]
    crows = rows // 2
    half = crows // 2
    edge_rows = CSTEPS
    coarse_tau = time_step * FSTEPS / CSTEPS

    has_up, has_low = s > 0, s < n_s - 1
    has_prev, has_next = t > 0, t < n_t - 1

    sources = (thick_hbm.at[0], bed_hbm, ice_hbm, zone_hbm)
    fields = (ha, bedx, icex, zonex)
    loads = []
    for f, (src, dst) in enumerate(zip(sources, fields)):
        for k in range(SUB):
            cp = pltpu.make_async_copy(
                src.at[:, k * width : (k + 1) * width], dst.at[fh : fh + rows, k, :], load_sem.at[f, k]
            )
            cp.start()
            loads.append(cp)

    partners = [
        (has_up, (t, s - 1)),
        (has_low, (t, s + 1)),
        (has_prev, (t - 1, s)),
        (has_next, (t + 1, s)),
    ]
    barrier = pltpu.get_barrier_semaphore()
    for cond, device in partners:
        @pl.when(cond)
        def _(device=device):
            pl.semaphore_signal(barrier, inc=1, device_id=device, device_id_type=MESH)
    sides = has_up.astype(jnp.int32) + has_low.astype(jnp.int32)
    slices = has_prev.astype(jnp.int32) + has_next.astype(jnp.int32)
    pl.semaphore_wait(barrier, sides + slices)

    @pl.when(has_prev)
    def _():
        pl.semaphore_signal(ready_sem, inc=1, device_id=(t - 1, s), device_id_type=MESH)

    for cp in loads:
        cp.wait()

    def remote(src, dst, ssem, rsem, device):
        return pltpu.make_async_remote_copy(
            src_ref=src, dst_ref=dst, send_sem=ssem, recv_sem=rsem, device_id=device, device_id_type=MESH
        )

    depth = (fh, fh, fh - 2, fh - 2)

    def halo_copy(side, f):
        ref, n = fields[f], depth[f]
        if side == 0:
            src, dst, device = ref.at[fh : fh + n], ref.at[fh + rows : fh + rows + n], (t, s - 1)
        else:
            src, dst, device = ref.at[fh + rows - n : fh + rows], ref.at[fh - n : fh], (t, s + 1)
        return remote(src, dst, halo_send.at[side, f], halo_recv.at[side, f], device)

    for side, cond in ((0, has_up), (1, has_low)):
        @pl.when(cond)
        def _(side=side):
            for f in range(len(fields)):
                halo_copy(side, f).start()

    def look_rows(start, count):
        store(ground, start, [lookup(x, levels_ref) for x in load(bedx, start, count)])
        store(gain, start, [time_step * lookup(x, rates_ref) for x in load(zonex, start, count)])
        store(cover, start, [x.astype(jnp.float32) for x in load(icex, start, count)])

    def coarsen(start, count):
        half = start // 2 if isinstance(start, int) else lax.div(start, 2)
        store(cground, half, restrict(load(ground, start, count)))
        store(ccover, half, restrict(load(cover, start, count)))
        store(cgain, half, [x * (coarse_tau / time_step) for x in restrict(load(gain, start, count))])
        store(cga, half, restrict(load(ha, start, count)))

    chain = (ha, hb, hc, hb, hc)
    fine = hc

    def fine_sweep(step, first, count):
        sweep(chain[step], chain[step + 1], ground, cover, gain, first, count, 1, 1.0, time_step)

    def coarse_sweep(src, dst, first, count):
        sweep(src, dst, cground, ccover, cgain, first, count, 2, 2.0, coarse_tau)

    def jump_rows(row, count):
        fine_mean = restrict(load(fine, 2 * row, 2 * count))
        store(jump, row, each(jnp.subtract, fine_mean, load(prev, row, count)))

    def end_copy(piece, start, count, slot):
        return remote(
            fine.at[pl.ds(fh + start, count)], prev_end.at[pl.ds(start, count)],
            end_send.at[piece], end_recv.at[piece], (slot, s),
        )

    end_pieces = ((0, fh, rows - 2 * fh), (1, rows - fh, fh), (2, 0, fh))

    def own_rows(i, carry):
        start = fh + i * 8
        look_rows(start, 8)
        coarsen(start, 8)
        return carry

    lax.fori_loop(0, rows // 8, own_rows, 0)

    for step in range(FSTEPS):
        edge = 2 * (step + 1)
        fine_sweep(step, fh + edge, rows - 2 * edge)

    @pl.when(has_next)
    def _():
        end_copy(*end_pieces[0], t + 1).start()

    coarse_sweep(cga, cgb, ch + 2, crows - 4)
    coarse_sweep(cgb, prev, ch + 4, crows - 8)
    jump_rows(2 * ch, crows - 2 * ch)

    def one_side(j, carry):
        side = lax.rem(s + j, 2)
        upper = side == 1

        def pick(up, low):
            return jnp.where(upper, up, low)

        start = pick(0, fh + rows)
        there = (upper & has_up) | (jnp.logical_not(upper) & has_low)

        @pl.when(there)
        def _():
            for f in range(len(fields)):
                n = depth[f]
                ref = fields[f].at[pl.ds(pick(fh - n, fh + rows), n)]
                remote(ref, ref, halo_send.at[side, f], halo_recv.at[side, f], (t, pick(s - 1, s + 1))).wait_recv()
            look_rows(start, fh)

        @pl.when(jnp.logical_not(there))
        def _():
            for ref in (ha, ground, cover, gain):
                zero = jnp.zeros((fh, SUB, LANE), ref.dtype)
                store(ref, start, [zero] * (width // LANE))

        coarsen(start, fh)
        for step in range(FSTEPS):
            edge = 2 * (step + 1)
            fine_sweep(step, pick(edge, fh + rows - edge), fh)

        @pl.when(has_next & ((j == 0) | has_prev))
        def _():
            end_copy(1 + side, pick(0, rows - fh), fh, t + 1).start()

        coarse_sweep(cga, cgb, pick(2, ch + crows - 2), ch)
        coarse_sweep(cgb, prev, pick(4, ch + crows - 4), ch)
        jump_rows(pick(ch, crows), ch)
        return carry

    lax.fori_loop(0, 2, one_side, 0)

    def chain_copy(part, slot):
        src = (pout, edge_out.at[0], edge_out.at[1])[part]
        dst = (pcur.at[ch : ch + half], edge_in.at[0], edge_in.at[1])[part]
        return remote(src, dst, chain_send.at[part], chain_recv.at[part], (slot, (s, s - 1, s + 1)[part]))

    chain_conds = (has_next, has_next & has_up, has_next & has_low)

    def packed_rows(ref, row, count):
        return merge(load(ref, row, count), load(ref, row + half, count))

    store(pjump, 0, packed_rows(jump, ch, half))

    @pl.when(jnp.logical_not(has_prev))
    def _():
        store(ptmp, ch, packed_rows(prev, ch, half))

    @pl.when(has_prev)
    def _():
        for src, dst in ((cground, pground), (ccover, pcover), (cgain, pgain)):
            store(dst, 0, packed_rows(src, 0, half))
            store(dst, half, packed_rows(src, half, 2 * ch))

    def finish(fine_ref, fine_at, current_ref, current_at, out_ref):
        def body(i, carry):
            p = load(current_ref, current_at + 4 * i, 4)
            top = merge(p, [to_odd(x) for x in p])
            low = merge([to_even(x) for x in p], p)
            for current, at in ((top, 8 * i), (low, 2 * half + 8 * i)):
                e = load(fine_ref, fine_at + at, 8)
                diff = each(jnp.subtract, current, restrict(e))
                store(out_ref, at, each(jnp.add, e, prolong(diff)))
            return carry

        lax.fori_loop(0, half // 4, body, 0)

    def write_out(buf, at, out, slot):
        return [
            pltpu.make_async_copy(
                buf.at[at : at + rows, k, :], out.at[0, :, k * width : (k + 1) * width], out_sem.at[slot, k]
            )
            for k in range(SUB)
        ]

    next_writes = write_out(next_buf, 0, next_hbm, 1)

    def next_state():
        @pl.when(has_prev)
        def _():
            for piece in end_pieces:
                end_copy(*piece, t - 1).wait_recv()
            finish(prev_end, 0, pcur, ch, next_buf)

        @pl.when(jnp.logical_not(has_prev))
        def _():
            next_buf[...] = ha[fh : fh + rows]

        for cp in next_writes:
            cp.start()

    @pl.when(has_prev)
    def _():
        for part, cond in ((1, has_low), (2, has_up)):
            @pl.when(jnp.logical_not(cond))
            def _(part=part):
                edge_in[part - 1] = jnp.zeros(edge_in.shape[1:], jnp.float32)

        chain_copy(0, t - 1).wait_recv()
        for part, cond in ((1, has_low), (2, has_up)):
            @pl.when(cond)
            def _(part=part):
                chain_copy(part, t - 1).wait_recv()

        low, up = (load(edge_in.at[side], 0, edge_rows) for side in range(2))
        inner = load(pcur, half, ch)
        upper = [jnp.concatenate([x, to_even(x)], axis=0) for x in up]
        store(pcur, 0, merge(upper, [to_odd(x) for x in inner]))
        inner = load(pcur, ch, ch)
        lower = [jnp.concatenate([to_odd(x), x], axis=0) for x in low]
        store(pcur, ch + half, merge([to_even(x) for x in inner], lower))

        @pl.when(jnp.logical_not(has_next))
        def _():
            next_state()

        sweep(pcur, cgb, pground, pcover, pgain, 2, half + 2 * ch - 4, 2, 2.0, coarse_tau)
        sweep(cgb, ptmp, pground, pcover, pgain, ch, half, 2, 2.0, coarse_tau)

    value = each(jnp.add, load(ptmp, ch, half), load(pjump, 0, half))
    store(pout, 0, value)
    n = edge_rows
    store(edge_out.at[0], 0, merge([x[:n] for x in value], [to_odd(x[n : 2 * n]) for x in value]))
    store(edge_out.at[1], 0, merge([to_even(x[-2 * n : -n]) for x in value], [x[-n:] for x in value]))

    @pl.when(has_next)
    def _():
        pl.semaphore_wait(ready_sem, 1)

    for part in (1, 2, 0):
        @pl.when(chain_conds[part])
        def _(part=part):
            chain_copy(part, t + 1).start()

    last_side = lax.rem(s + 1, 2)

    @pl.when(has_next & jnp.logical_not(has_prev))
    def _():
        end_copy(1 + last_side, jnp.where(last_side == 1, 0, rows - fh), fh, t + 1).start()

    finish(fine, fh, pout, 0, end_buf)
    end_writes = write_out(end_buf, 0, end_hbm, 0)
    for cp in end_writes:
        cp.start()

    @pl.when(has_next)
    def _():
        next_state()

    for side, cond in ((0, has_up), (1, has_low)):
        @pl.when(cond)
        def _(side=side):
            for f in range(len(fields)):
                halo_copy(side, f).wait_send()
    for part, cond in enumerate(chain_conds):
        @pl.when(cond)
        def _(part=part):
            chain_copy(part, t + 1).wait_send()

    @pl.when(has_next)
    def _():
        for piece in end_pieces:
            end_copy(*piece, t + 1).wait_send()

    for cp in end_writes + next_writes:
        cp.wait()


def per_device(thickness, bed_class, ice_mask, zone_index, bed_levels, balance_rates):
    _, rows, cols = thickness.shape
    width = cols // SUB
    crows = rows // 2
    fx, cx, px = rows + 4 * FSTEPS, crows + 4 * CSTEPS, crows // 2 + 4 * CSTEPS

    def buf(count, dtype=jnp.float32):
        return pltpu.VMEM((count, SUB, width), dtype)

    dma = pltpu.SemaphoreType.DMA
    shape = jax.ShapeDtypeStruct(thickness.shape, jnp.float32)
    return pl.pallas_call(
        kernel,
        out_shape=(shape, shape),
        in_specs=[pl.BlockSpec(memory_space=pl.ANY)] * 4 + [pl.BlockSpec(memory_space=pltpu.SMEM)] * 2,
        out_specs=(pl.BlockSpec(memory_space=pl.ANY), pl.BlockSpec(memory_space=pl.ANY)),
        scratch_shapes=[
            buf(fx), buf(fx), buf(fx),
            buf(fx, jnp.int32), buf(fx, jnp.int32), buf(fx, jnp.int32),
            buf(fx), buf(fx), buf(fx),
            buf(cx), buf(cx), buf(cx), buf(cx), buf(cx), buf(cx), buf(cx),
            buf(px), buf(px), buf(px), buf(crows // 2), buf(px), buf(px), buf(crows // 2),
            pltpu.VMEM((2, CSTEPS, SUB, width), jnp.float32), pltpu.VMEM((2, CSTEPS, SUB, width), jnp.float32),
            buf(rows), buf(rows), buf(rows),
            dma((4, SUB)), dma((2, 4)), dma((2, 4)), dma((3,)), dma((3,)), dma((3,)), dma((3,)), dma((2, SUB)), pltpu.SemaphoreType.REGULAR,
        ],
        compiler_params=pltpu.CompilerParams(collective_id=0, has_side_effects=True),
    )(thickness, bed_class, ice_mask, zone_index, bed_levels, balance_rates)


def solution(mesh):
    placed = (
        P("tm", "space", None),
        P("space", None),
        P("space", None),
        P("space", None),
        P(),
        P(),
    )
    return jax.shard_map(
        per_device,
        mesh=mesh,
        in_specs=placed,
        out_specs=(P("tm", "space", None), P("tm", "space", None)),
        check_vma=False,
    )
```
